32 devices in a mesh: term: 8 (over z, y), sec: 4 (over x, core).
Axes of the slice: x: 2, y: 2, z: 4, core: 2. Of those that a mesh axis runs over, the one named last changes fastest.
Arguments:
- state: bfloat16 [4, 768, 768], P('sec'), may hold values from -6 to 6
- left_environment: bfloat16 [8, 4, 768, 768], P('term', 'sec'), may hold values from -0.21875 to 0.21875
- right_environment: bfloat16 [8, 4, 768, 768], P('term', 'sec'), may hold values from -0.21875 to 0.21875
- site_blocks: bfloat16 [4, 768, 768], P('sec'), may hold values from -3 to 3
- sector_sizes: int32 [4], replicated, may hold values from 192 to 768, as said below
- term_shift: int32 [8], P('term'), may hold values from -1 to 1
Outputs:
- applied: float32 [4, 768, 768], P('sec', 'term')
- new_left: bfloat16 [8, 4, 768, 768], P('term', 'sec')
The draws below stay inside these ranges and needn't reach their ends.
Inputs may be any that keep to these rules, and one draw needn't show every extreme that they name: `sector_sizes`: every sector holds at least 192 states and the largest sector holds exactly 768.
All inputs are finite; a program needn't handle non-finite values.
Results may differ from the reference program's by a relative error of at most 0.0049.
Values may be sent and summed in bfloat16 or wider, within the bound.
A program may use at most 64 MiB of HBM per device.

```python
import jax
import jax.numpy as jnp
from jax import lax

M = 768
NSEC = 4
NTERM = 8


def draw_sector_sizes(key, part):
    first_key, second_key = jax.random.split(jax.random.fold_in(key, 11))
    counts = jax.random.randint(first_key, (NSEC,), M // 4, M + 1)
    largest = jax.random.randint(second_key, (), 0, NSEC)
    return counts.at[largest].set(M).astype(jnp.int32)


def touch_ends(entries, stream_key, least, top_value):
    longest = entries.shape.index(max(entries.shape))
    spots = []
    for shift in (0, 1):
        where = [jax.random.randint(jax.random.fold_in(stream_key, axis), (), 0, length) for axis, length in enumerate(entries.shape)]
        where[longest] = (where[longest] + shift) % entries.shape[longest]
        spots.append(tuple(where))
    return entries.at[spots[0]].set(least).at[spots[1]].set(top_value)


def block_levels(stream_key, dims, cuts, least, high):
    loudness, own = 1.0, jax.random.fold_in(stream_key, 6)
    for dim, blocks in cuts:
        steps = jnp.exp(jax.random.uniform(jax.random.fold_in(own, dim), (blocks,), jnp.float32, least / len(cuts), high / len(cuts)))
        loudness = loudness * jnp.repeat(steps, dims[dim] // blocks).reshape([-1 if axis == dim else 1 for axis in range(len(dims))])
    return loudness


def noise(key, shape, width, most, cuts=(), held_as=jnp.bfloat16):
    level = block_levels(key, shape, cuts, -0.22, 0.18) if cuts else 1.0
    values = jax.random.normal(key, shape, jnp.float32) * width * level
    return jnp.minimum(jnp.maximum(values, -most), most).astype(held_as)


def setup_inputs(seed: int = 0) -> dict:
    streams_of = jax.random.split(jax.random.key(seed), 7)
    return {
        "state": noise(streams_of[0], (NSEC, M, M), 1.0, 6.0, ((0, 4),)),
        "left_environment": noise(streams_of[1], (NTERM, NSEC, M, M), M ** -0.5, 0.21875, ((0, 8), (1, 4))),
        "right_environment": noise(streams_of[2], (NTERM, NSEC, M, M), M ** -0.5, 0.21875, ((0, 8), (1, 4))),
        "site_blocks": noise(streams_of[3], (NSEC, M, M), (M ** -0.25), 3.0, ((0, 4),)),
        "sector_sizes": draw_sector_sizes(jax.random.fold_in(streams_of[6], 71), 0),
        "term_shift": touch_ends(jax.random.randint(streams_of[5], (NTERM,), -1, 2), jax.random.fold_in(streams_of[5], 1), -1, 1).astype(jnp.int32),
    }


def shifted(padded, charge_shift):
    return lax.dynamic_slice_in_dim(padded, (charge_shift + 1).astype(jnp.int32), NSEC, 0)


def reference(state, left_environment, right_environment, site_blocks, sector_sizes, term_shift):
    row_index = jnp.arange(M, dtype=jnp.int32)
    valid_rows = (row_index[None, :] < sector_sizes[:, None]).astype(jnp.float32)
    both = valid_rows[:, :, None] * valid_rows[:, None, :]
    masked_state = state.astype(jnp.float32) * both
    masked_site = site_blocks.astype(jnp.float32) * both
    empty = jnp.zeros((1, M, M), jnp.float32)
    state_padded = jnp.concatenate([empty, masked_state, empty], axis=0)
    site_padded = jnp.concatenate([empty, masked_site, empty], axis=0)
    valid_padded = jnp.concatenate([jnp.zeros((1, M), jnp.float32), valid_rows, jnp.zeros((1, M), jnp.float32)], axis=0)
    highest = lax.Precision.HIGHEST

    def one_term(total, inputs):
        left_term, right_term, charge_shift = inputs
        source_valid = shifted(valid_padded, charge_shift)
        source_state = shifted(state_padded, charge_shift)
        source_site = shifted(site_padded, charge_shift)
        left_masked = left_term.astype(jnp.float32) * valid_rows[:, :, None] * source_valid[:, None, :]
        right_masked = right_term.astype(jnp.float32) * source_valid[:, :, None] * valid_rows[:, None, :]
        mixed_block = jnp.einsum("sij,sjk->sik", source_state, right_masked, precision=highest)
        mixed_block = mixed_block.astype(jnp.bfloat16).astype(jnp.float32)
        partial_rows = jnp.einsum("sij,sjk->sik", left_masked, mixed_block, precision=highest)
        carried = jnp.einsum("sij,sjk->sik", left_masked, source_site, precision=highest)
        carried = carried.astype(jnp.bfloat16).astype(jnp.float32)
        renewed = jnp.einsum("sji,sjk->sik", masked_site, carried, precision=highest).astype(jnp.bfloat16)
        return total + partial_rows, renewed

    applied, new_left = lax.scan(one_term, jnp.zeros((NSEC, M, M), jnp.float32), (left_environment, right_environment, term_shift))
    return applied, new_left
```

```python
import functools

import jax
import jax.numpy as jnp
from jax import lax
from jax.experimental import pallas as pl
from jax.experimental.pallas import tpu as pltpu
from jax.sharding import PartitionSpec as P

MESH = pl.DeviceIdType.MESH
BF16 = jnp.bfloat16
F32 = jnp.float32
CHUNKS = 4
BY_Y = 2
SHARE = 8


def pick(number, table):
    out = jnp.int32(table[0])
    for i, entry in enumerate(table):
        if i:
            out = jnp.where(number == i, entry, out)
    return out


def helps_below(z):
    return z % 2 == 0


def plan(z, depth):
    mate = z + 1 - 2 * (z % 2)
    sums = [d for d in range(depth) if d not in (z, mate) and (d < z) == helps_below(z)]
    hands = [d for d in range(depth) if d != z and d not in sums]
    farther = lambda d: -abs(d - z)
    return sorted(hands, key=farther), sorted(sums, key=farther)


def kernel(
    terms, sectors,
    state, left, right, site, sizes_there, shift_there,
    applied, new_left,
    own_s, own_b, lm, rm, mate_s, far_s, mate_b, far_b, bt, mixed, weight,
    acc, kept, y_send, y_recv, z_send, z_recv,
    sizes, shift, local_sem, mate_send, mate_recv, x_send_sem, x_recv_sem, relay_send, relay_recv,
    y_send_sem, y_recv_sem, z_send_sem, z_recv_sem,
):
    width = own_s.shape[0]
    depth = terms // 2
    rows = width // terms
    pieces, rows_of_piece = y_send.shape[1], y_send.shape[2]
    quarter = width // 4
    chunk = quarter // CHUNKS
    share = width // SHARE
    t, p = lax.axis_index("term"), lax.axis_index("sec")
    z, y = t // 2, t % 2
    odd = p % 2
    mate = p + 1 - 2 * odd
    far = p - 1 + 2 * odd
    has_far = jnp.logical_and(far >= 0, far < sectors)
    far_there = lax.rem(far + sectors, sectors)
    zlow = z % 2
    pair = z // 2
    y_peer = 2 * z + 1 - y
    z_near = 2 * (z + 1 - 2 * zlow) + y
    plans = [plan(i, depth) for i in range(depth)]
    handed = pick(z, [len(hands) for hands, sums in plans])
    order = [pick(z, [(hands + sums + [i])[k] for i, (hands, sums) in enumerate(plans)]) for k in range(depth)]
    summed = [k >= handed for k in range(depth - 1)]

    loads = [
        pltpu.make_async_copy(state.at[0], own_s, local_sem.at[0]),
        pltpu.make_async_copy(left.at[0, 0], lm, local_sem.at[1]),
        pltpu.make_async_copy(right.at[0, 0], rm, local_sem.at[2]),
        pltpu.make_async_copy(site.at[0], own_b, local_sem.at[3]),
        pltpu.make_async_copy(sizes_there, sizes, local_sem.at[4]),
        pltpu.make_async_copy(shift_there, shift, local_sem.at[5]),
    ]

    barrier = pltpu.get_barrier_semaphore()
    pl.semaphore_signal(barrier, inc=1, device_id=(t, mate), device_id_type=MESH)

    @pl.when(has_far)
    def _():
        pl.semaphore_signal(barrier, inc=1, device_id=(t, far_there), device_id_type=MESH)

    pl.semaphore_signal(barrier, inc=1, device_id=(y_peer, p), device_id_type=MESH)
    pl.semaphore_signal(barrier, inc=1, device_id=(z_near, p), device_id_type=MESH)
    for other in range(depth // 2):
        @pl.when(other != pair)
        def _():
            closest = 2 * other + jnp.where(other < pair, 1, 0)
            pl.semaphore_signal(
                barrier, inc=1, device_id=(2 * closest + y, p), device_id_type=MESH
            )

    for load in loads:
        load.start()

    @pl.when(jnp.logical_not(has_far))
    def _():
        far_s[...] = jnp.zeros_like(far_s)
        far_b[...] = jnp.zeros_like(far_b)

    pl.semaphore_wait(barrier, 3 + (depth - 1 - handed) + jnp.where(has_far, 1, 0))

    def remote(src, dst, send, recv, device):
        return pltpu.make_async_remote_copy(
            src_ref=src, dst_ref=dst, send_sem=send, recv_sem=recv,
            device_id=device, device_id_type=MESH,
        )

    def part(number, first=0, count=CHUNKS):
        return pl.ds(pl.multiple_of(number * quarter + first * chunk, chunk), count * chunk)

    q_own = 2 * zlow + y
    q_y = 2 * zlow + 1 - y
    q_z = 2 * (1 - zlow) + y
    q_d = 2 * (1 - zlow) + 1 - y
    there = (t, far_there)

    x_count = 0

    def cross(array, target, where):
        nonlocal x_count
        copy = remote(
            array.at[0, where], target.at[where],
            x_send_sem.at[x_count], x_recv_sem.at[x_count], there,
        )
        x_count += 1
        return copy

    relay_count = 0

    def relay(target, where, arrives, device):
        nonlocal relay_count
        there_and_back = [
            remote(
                target.at[rows_there], target.at[rows_there],
                relay_send.at[relay_count], relay_recv.at[relay_count], device,
            )
            for rows_there in (where, arrives)
        ]
        relay_count += 1
        return there_and_back

    x_own = [cross(state, far_s, part(q_own, c, 1)) for c in range(CHUNKS)]
    x_diagonal = cross(state, far_s, part(q_d))
    x_beside = [cross(state, far_s, part(q_y, BY_Y, CHUNKS - BY_Y))] if BY_Y < CHUNKS else []
    by_y = [relay(far_s, part(q_own, c, 1), part(q_y, c, 1), (y_peer, p)) for c in range(BY_Y)]
    by_z = [relay(far_s, part(q_own, c, 1), part(q_z, c, 1), (z_near, p)) for c in range(CHUNKS)]
    late = 2 * (width // 3)
    mine = pl.ds(pl.multiple_of(zlow * share, share), share)
    theirs = pl.ds(pl.multiple_of((1 - zlow) * share, share), share)
    x_site = [
        cross(site, far_b, mine),
        cross(site, far_b, pl.ds(2 * share, late - 2 * share)),
        cross(site, far_b, pl.ds(late, width - late)),
    ]
    site_by_z = relay(far_b, mine, theirs, (z_near, p))
    mate_copies = [
        remote(
            state.at[0, part(q)], mate_s.at[part(q)], mate_send.at[i], mate_recv.at[i],
            (t, mate),
        )
        for i, q in enumerate((q_own, q_d, q_z, q_y))
    ]
    mate_site = remote(site.at[0], mate_b, mate_send.at[4], mate_recv.at[4], (t, mate))

    @pl.when(has_far)
    def _():
        for copy in x_own + [x_diagonal] + x_beside + x_site:
            copy.start()

    for copy in mate_copies + [mate_site]:
        copy.start()

    loads[4].wait()
    loads[5].wait()
    charge_shift = shift[0]
    own_size = jnp.int32(0)
    source_size = jnp.int32(0)
    for i in range(sectors):
        own_size = own_size + jnp.where(p == i, sizes[i], 0)
        source_size = source_size + jnp.where(p + charge_shift == i, sizes[i], 0)
    towards = charge_shift * (1 - 2 * odd)

    def choose(own, near, away):
        return jnp.where(towards == 0, own, jnp.where(towards == 1, near, away))

    loads[2].wait()
    row_ids = lax.broadcasted_iota(jnp.int32, (width, 1), 0)
    rm[...] = rm[...] * jnp.where(row_ids < source_size, 1.0, 0.0).astype(BF16)
    loads[1].wait()
    col_ids = lax.broadcasted_iota(jnp.int32, (1, width), 1)
    lm[...] = lm[...] * jnp.where(col_ids < source_size, 1.0, 0.0).astype(BF16)
    loads[3].wait()
    own_rows = (row_ids < own_size).astype(F32)

    def weigh(i):
        where = pl.ds(i * quarter, quarter)
        weight[where, :] = jnp.dot(
            bt[where, :], lm[...], preferred_element_type=F32
        ).astype(BF16)

    def weigh_all():
        bt[...] = (own_b[...] * own_rows.astype(BF16)).T
        for i in range(4):
            weigh(i)

    @pl.when(has_far)
    def _():
        bt[...] = (own_b[...] * own_rows.astype(BF16)).T
        for c in range(CHUNKS):
            x_own[c].wait_recv()
            if c < BY_Y:
                by_y[c][0].start()
            by_z[c][0].start()
            if c < 4:
                weigh(c)
        for c in range(CHUNKS, 4):
            weigh(c)

    loads[0].wait()

    def mix(i, number):
        mate_copies[i].wait_recv()
        where = part(number)
        source = choose(own_s[where, :], mate_s[where, :], far_s[where, :])
        mixed[where, :] = jnp.dot(source, rm[...], preferred_element_type=F32).astype(BF16)

    mix(0, q_own)

    @pl.when(has_far)
    def _():
        x_diagonal.wait_recv()

    mix(1, q_d)

    @pl.when(has_far)
    def _():
        for copy in by_z:
            copy[1].wait_recv()

    mix(2, q_z)

    @pl.when(has_far)
    def _():
        for copy in by_y:
            copy[1].wait_recv()
        for copy in x_beside:
            copy.wait_recv()

    mix(3, q_y)

    y_copies, z_copies = [], []
    for k in range(depth):
        start = order[k] * 2 * rows
        give = pl.ds(pl.multiple_of(start + (1 - y) * rows, rows), rows)
        keep = pl.ds(pl.multiple_of(start + y * rows, rows), rows)
        both = jnp.dot(
            jnp.concatenate([lm[give, :], lm[keep, :]], axis=0), mixed[...],
            preferred_element_type=F32,
        )
        y_copies.append([])
        for i in range(pieces):
            y_send[k, i] = both[i * rows_of_piece:(i + 1) * rows_of_piece].astype(BF16)
            copy = remote(
                y_send.at[k, i], y_recv.at[k, i], y_send_sem.at[k, i], y_recv_sem.at[k, i],
                (y_peer, p),
            )
            copy.start()
            y_copies[k].append(copy)
        for i in range(pieces):
            kept[k, i] = both[rows + i * rows_of_piece:rows + (i + 1) * rows_of_piece]

    @pl.when(jnp.logical_not(has_far))
    def _():
        weigh_all()

    @pl.when(has_far)
    def _():
        x_site[0].wait_recv()
        site_by_z[0].start()

    def arrival(slot, i):
        return remote(
            z_send.at[0, i], z_recv.at[slot, i], z_send_sem.at[0, i], z_recv_sem.at[slot, i],
            (z_near, p),
        )

    for k in range(depth - 1):
        for i in range(pieces):
            y_copies[k][i].wait_recv()
            kept[k, i] = kept[k, i] + y_recv[k, i].astype(F32)

            @pl.when(summed[k])
            def _():
                arrival(order[k], i).wait_recv()
                kept[k, i] = kept[k, i] + z_recv[order[k], i].astype(F32)

            z_send[k, i] = kept[k, i].astype(BF16)
            slot = jnp.where(summed[k], depth + pair, order[k])
            peer = jnp.where(summed[k], 2 * order[k] + y, z_near)
            copy = remote(
                z_send.at[k, i], z_recv.at[slot, i], z_send_sem.at[k, i],
                z_recv_sem.at[slot, i], (peer, p),
            )
            copy.start()
            z_copies.append(copy)

    mate_site.wait_recv()

    @pl.when(has_far)
    def _():
        site_by_z[1].wait_recv()
        x_site[1].wait_recv()

    early = pl.ds(0, late)
    own_b[early, :] = choose(own_b[early, :], mate_b[early, :], far_b[early, :])
    for i in range(4):
        where = pl.ds(i * quarter, quarter)
        acc[where, :] = jnp.dot(
            weight[where, early], own_b[early, :], preferred_element_type=F32
        )

    last = depth - 1
    for i in range(pieces):
        y_copies[last][i].wait_recv()
        kept[last, i] = kept[last, i] + y_recv[last, i].astype(F32)

    @pl.when(has_far)
    def _():
        x_site[2].wait_recv()

    rest = pl.ds(late, width - late)
    lane_mask = (col_ids < source_size).astype(F32)
    tail = choose(own_b[rest, :], mate_b[rest, :], far_b[rest, :])
    for i in range(4):
        where = pl.ds(i * quarter, quarter)
        renewed = acc[where, :] + jnp.dot(
            weight[where, rest], tail, preferred_element_type=F32
        )
        ids = lax.broadcasted_iota(jnp.int32, (quarter, 1), 0) + i * quarter
        renewed = renewed * lane_mask * (ids < own_size).astype(F32)
        new_left[0, 0, where, :] = renewed.astype(BF16)

    keep_cols = (col_ids < own_size).astype(F32)
    for i in range(pieces):
        arrival(z, i).wait_recv()
        kept[last, i] = kept[last, i] + z_recv[z, i].astype(F32)
        for other in range(depth // 2):
            @pl.when(other != pair)
            def _():
                arrival(depth + other, i).wait_recv()
                kept[last, i] = kept[last, i] + z_recv[depth + other, i].astype(F32)

        ids = lax.broadcasted_iota(jnp.int32, (rows_of_piece, 1), 0) + t * rows + i * rows_of_piece
        keep_rows = (ids < own_size).astype(F32)
        applied[0, pl.ds(i * rows_of_piece, rows_of_piece)] = kept[last, i] * keep_rows * keep_cols

    for copies in y_copies:
        for copy in copies:
            copy.wait_send()
    for copy in z_copies + mate_copies + [mate_site]:
        copy.wait_send()

    @pl.when(has_far)
    def _():
        for copy in x_own + [x_diagonal] + x_beside + x_site:
            copy.wait_send()
        for copy in by_y + by_z + [site_by_z]:
            copy[0].wait_send()


def write_out(applied, new_left, applied_there, new_left_there, sem):
    copies = [
        pltpu.make_async_copy(new_left, new_left_there, sem.at[0]),
        pltpu.make_async_copy(applied, applied_there, sem.at[1]),
    ]
    for copy in copies:
        copy.start()
    for copy in copies:
        copy.wait()


def shards(terms, sectors, state, left_environment, right_environment, site_blocks,
           sector_sizes, term_shift):
    width = state.shape[1]
    rows = width // terms
    depth = terms // 2
    pieces = 2 if rows % 32 == 0 else 1
    square = pltpu.VMEM((width, width), BF16)
    hbm = pl.BlockSpec(memory_space=pltpu.HBM)
    vmem = pl.BlockSpec(memory_space=pltpu.VMEM)
    dma = pltpu.SemaphoreType.DMA

    def blocks(count, dtype):
        return pltpu.VMEM((count, pieces, rows // pieces, width), dtype)

    outs = (
        ((1, rows, width), F32),
        ((1, 1, width, width), BF16),
    )
    results = pl.pallas_call(
        functools.partial(kernel, terms, sectors),
        out_shape=tuple(pltpu.VMEM(shape, dtype) for shape, dtype in outs),
        in_specs=[hbm] * 6,
        out_specs=(vmem, vmem),
        scratch_shapes=[square] * 11 + [
            pltpu.VMEM((width, width), F32),
            blocks(depth, F32),
            blocks(depth, BF16),
            blocks(depth, BF16),
            blocks(depth, BF16),
            blocks(depth + depth // 2, BF16),
            pltpu.SMEM((sectors,), jnp.int32), pltpu.SMEM((1,), jnp.int32),
            dma((6,)), dma((5,)), dma((5,)), dma((CHUNKS + 6,)), dma((CHUNKS + 6,)),
            dma((2 * CHUNKS + 2,)), dma((2 * CHUNKS + 2,)),
            dma((depth, pieces)), dma((depth, pieces)), dma((depth, pieces)),
            dma((depth + depth // 2, pieces)),
        ],
        compiler_params=pltpu.CompilerParams(
            collective_id=0, has_side_effects=True, vmem_limit_bytes=62500 * 1024
        ),
    )(state, left_environment, right_environment, site_blocks, sector_sizes, term_shift)
    return pl.pallas_call(
        write_out,
        out_shape=tuple(jax.ShapeDtypeStruct(shape, dtype) for shape, dtype in outs),
        in_specs=[vmem, vmem],
        out_specs=(hbm, hbm),
        scratch_shapes=[dma((2,))],
    )(*(pltpu.with_memory_space_constraint(result, pltpu.VMEM) for result in results))


def solution(mesh):
    placed = (
        P("sec", None, None),
        P("term", "sec", None, None),
        P("term", "sec", None, None),
        P("sec", None, None),
        P(),
        P("term"),
    )
    return jax.shard_map(
        functools.partial(shards, mesh.shape["term"], mesh.shape["sec"]),
        mesh=mesh,
        in_specs=placed,
        out_specs=(P("sec", "term", None), P("term", "sec", None, None)),
        check_vma=False,
    )
```

```python
import functools

import jax
import jax.numpy as jnp
from jax import lax
from jax.experimental import pallas as pl
from jax.experimental.pallas import tpu as pltpu
from jax.sharding import PartitionSpec as P

MESH = pl.DeviceIdType.MESH
BF16 = jnp.bfloat16
F32 = jnp.float32
CHUNKS = 4
BY_Y = 2
SHARE = 2
UPWARD = 1
BESIDE = 4
EARLY = 1
DIRECT = (0, 2)
RANK = (1, 0, 2)
WEIGH_FIRST = 0
PIECES = 2


def pick(number, table):
    out = jnp.int32(table[0])
    for i, entry in enumerate(table):
        if i:
            out = jnp.where(number == i, entry, out)
    return out


def hands_over(z, d, direct):
    if z // 2 == d // 2 or (z % 2 == 0) == (d < z):
        return False
    return direct == 0 or direct == 2 and (d % 2 == 1) == (d < z)


def plan(z, depth, direct):
    mate = z + 1 - 2 * (z % 2)
    steps = []
    for d in range(depth):
        if d != z:
            act = 1 if hands_over(z, d, direct) else 0
            if z // 2 != d // 2 and hands_over(mate, d, direct):
                act = 2
            steps.append((RANK[act], d if UPWARD else -abs(d - z), d, act))
    return [(d, act) for _, _, d, act in sorted(steps)]


def kernel(
    terms, sectors,
    state, left, right, site, sizes_there, shift_there,
    applied, new_left,
    own_s, own_b, lm, rm, mate_s, far_s, mate_b, far_b, bt, mixed, weight,
    acc, kept, y_send, y_recv, z_send, z_recv,
    sizes, shift, local_sem, mate_send, mate_recv, x_send_sem, x_recv_sem, relay_send, relay_recv,
    y_send_sem, y_recv_sem, z_send_sem, z_recv_sem, in_sem,
):
    width = own_s.shape[0]
    depth = terms // 2
    rows = width // terms
    pieces, rows_of_piece = y_send.shape[1], y_send.shape[2]
    quarter = width // 4
    chunk = quarter // CHUNKS
    share = width * SHARE // 24
    t, p = lax.axis_index("term"), lax.axis_index("sec")
    z, y = t // 2, t % 2
    odd = p % 2
    mate = p + 1 - 2 * odd
    far = p - 1 + 2 * odd
    has_far = jnp.logical_and(far >= 0, far < sectors)
    far_there = lax.rem(far + sectors, sectors)
    zlow = z % 2
    pair = z // 2
    y_peer = 2 * z + 1 - y
    z_near = 2 * (z + 1 - 2 * zlow) + y
    plans = [[plan(i, depth, direct) for i in range(depth)] for direct in DIRECT]

    def by_plan(table):
        near, away = (pick(z, [table(i, steps) for i, steps in enumerate(kind)]) for kind in plans)
        return jnp.where(has_far, away, near)

    def link_to(j):
        return by_plan(lambda i, steps: int(any(d == j and act != 1 for d, act in steps))) == 1

    def link_from(j):
        near, away = (
            pick(z, [int(any(d == i and act != 1 for d, act in kind[j])) for i in range(depth)])
            for kind in plans
        )
        return jnp.where(has_far, away, near) == 1

    order = [by_plan(lambda i, steps: steps[k][0]) for k in range(depth - 1)] + [z]
    acts = [by_plan(lambda i, steps: steps[k][1]) for k in range(depth - 1)]

    loads = [
        pltpu.make_async_copy(state.at[0], own_s, local_sem.at[0]),
        pltpu.make_async_copy(left.at[0, 0], lm, local_sem.at[1]),
        pltpu.make_async_copy(right.at[0, 0], rm, local_sem.at[2]),
        pltpu.make_async_copy(site.at[0], own_b, local_sem.at[3]),
        pltpu.make_async_copy(sizes_there, sizes, local_sem.at[4]),
        pltpu.make_async_copy(shift_there, shift, local_sem.at[5]),
    ]

    for load in loads:
        load.start()

    barrier = pltpu.get_barrier_semaphore()
    leads = far > p
    follows = jnp.logical_and(has_far, far < p)
    leads = jnp.logical_and(has_far, leads)

    def when(condition, act):
        @pl.when(condition)
        def _():
            act()

    def greet(condition, device):
        when(condition, lambda: pl.semaphore_signal(
            barrier, inc=1, device_id=device, device_id_type=MESH))

    def answer(condition, device, number):
        when(condition, lambda: pl.semaphore_signal(
            in_sem.at[number], inc=1, device_id=device, device_id_type=MESH))

    def hear(condition, number):
        when(condition, lambda: pl.semaphore_wait(in_sem.at[number], 1))

    greet(leads, (t, far_there))
    greet(odd == 1, (t, mate))
    greet(y == 0, (y_peer, p))
    greet(zlow == 0, (z_near, p))
    below = jnp.int32(0)
    for plane in range(depth):
        apart = plane // 2 != pair
        linked = jnp.logical_and(apart, jnp.logical_or(link_to(plane), link_from(plane)))
        greet(jnp.logical_and(linked, plane > z), (2 * plane + y, p))
        below = below + jnp.where(jnp.logical_and(linked, plane < z), 1, 0)
    greetings = jnp.where(follows, 1, 0) + (1 - odd) + y + zlow + below
    when(greetings > 0, lambda: pl.semaphore_wait(barrier, greetings))
    answer(follows, (t, far_there), 0)
    answer(odd == 0, (t, mate), 1)
    answer(y == 1, (y_peer, p), 2)
    answer(zlow == 1, (z_near, p), 3)
    for plane in range(depth):
        lower = jnp.logical_and(plane // 2 != pair, plane < z)
        answer(jnp.logical_and(lower, link_from(plane)), (2 * plane + y, p), 4 + z)

    def remote(src, dst, send, recv, device):
        return pltpu.make_async_remote_copy(
            src_ref=src, dst_ref=dst, send_sem=send, recv_sem=recv,
            device_id=device, device_id_type=MESH,
        )

    def part(number, first=0, count=CHUNKS):
        return pl.ds(pl.multiple_of(number * quarter + first * chunk, chunk), count * chunk)

    q_own = 2 * zlow + y
    q_y = 2 * zlow + 1 - y
    q_z = 2 * (1 - zlow) + y
    q_d = 2 * (1 - zlow) + 1 - y
    there = (t, far_there)

    x_count = 0

    def cross(array, target, where):
        nonlocal x_count
        copy = remote(
            array.at[0, where], target.at[where],
            x_send_sem.at[x_count], x_recv_sem.at[x_count], there,
        )
        x_count += 1
        return copy

    relay_count = 0

    def relay(target, where, arrives, device):
        nonlocal relay_count
        there_and_back = [
            remote(
                target.at[rows_there], target.at[rows_there],
                relay_send.at[relay_count], relay_recv.at[relay_count], device,
            )
            for rows_there in (where, arrives)
        ]
        relay_count += 1
        return there_and_back

    x_own = [cross(state, far_s, part(q_own, c, 1)) for c in range(CHUNKS)]
    x_diagonal = cross(state, far_s, part(q_d))
    x_beside = [cross(state, far_s, part(q_y, BY_Y, CHUNKS - BY_Y))] if BY_Y < CHUNKS else []
    by_y = [relay(far_s, part(q_own, c, 1), part(q_y, c, 1), (y_peer, p)) for c in range(BY_Y)]
    by_z = [relay(far_s, part(q_own, c, 1), part(q_z, c, 1), (z_near, p)) for c in range(CHUNKS)]
    late = 2 * (width // 3)
    mine = pl.ds(pl.multiple_of(zlow * share, share), share)
    theirs = pl.ds(pl.multiple_of((1 - zlow) * share, share), share)
    beside = width * BESIDE // 24
    mine_y = pl.ds(pl.multiple_of(late + y * beside, 16), beside)
    theirs_y = pl.ds(pl.multiple_of(late + (1 - y) * beside, 16), beside)
    left_over = width - late - 2 * beside
    site_z = cross(site, far_b, mine)
    site_y = cross(site, far_b, mine_y)
    site_early = cross(site, far_b, pl.ds(2 * share, late - 2 * share))
    site_late = [cross(site, far_b, pl.ds(width - left_over, left_over))] if left_over else []
    x_site = [site_z, site_y, site_early] + site_late
    site_by_z = relay(far_b, mine, theirs, (z_near, p))
    site_by_y = relay(far_b, mine_y, theirs_y, (y_peer, p))
    mate_copies = [
        remote(
            state.at[0, part(q)], mate_s.at[part(q)], mate_send.at[i], mate_recv.at[i],
            (t, mate),
        )
        for i, q in enumerate((q_own, q_d, q_z, q_y))
    ]
    mate_site = remote(site.at[0], mate_b, mate_send.at[4], mate_recv.at[4], (t, mate))

    def send_far():
        for copy in x_own + [x_diagonal] + x_beside + x_site:
            copy.start()

    when(follows, send_far)
    hear(odd == 1, 1)
    for copy in mate_copies + [mate_site]:
        copy.start()
    if EARLY:
        hear(leads, 0)
        when(leads, send_far)
    @pl.when(jnp.logical_not(has_far))
    def _():
        far_s[...] = jnp.zeros_like(far_s)
        far_b[...] = jnp.zeros_like(far_b)


    loads[4].wait()
    loads[5].wait()
    charge_shift = shift[0]
    own_size = jnp.int32(0)
    source_size = jnp.int32(0)
    for i in range(sectors):
        own_size = own_size + jnp.where(p == i, sizes[i], 0)
        source_size = source_size + jnp.where(p + charge_shift == i, sizes[i], 0)
    towards = charge_shift * (1 - 2 * odd)

    def choose(own, near, away):
        return jnp.where(towards == 0, own, jnp.where(towards == 1, near, away))

    loads[2].wait()
    row_ids = lax.broadcasted_iota(jnp.int32, (width, 1), 0)
    rm[...] = rm[...] * jnp.where(row_ids < source_size, 1.0, 0.0).astype(BF16)
    loads[1].wait()
    col_ids = lax.broadcasted_iota(jnp.int32, (1, width), 1)
    lm[...] = lm[...] * jnp.where(col_ids < source_size, 1.0, 0.0).astype(BF16)
    if not EARLY:
        hear(leads, 0)
        when(leads, send_far)
    loads[3].wait()
    own_rows = (row_ids < own_size).astype(F32)

    def weigh(i):
        where = pl.ds(i * quarter, quarter)
        weight[where, :] = jnp.dot(
            bt[where, :], lm[...], preferred_element_type=F32
        ).astype(BF16)

    def weigh_all():
        bt[...] = (own_b[...] * own_rows.astype(BF16)).T
        for i in range(4):
            weigh(i)

    @pl.when(has_far)
    def _():
        bt[...] = (own_b[...] * own_rows.astype(BF16)).T
        hear(y == 0, 2)
        hear(zlow == 0, 3)
        for c in range(CHUNKS):
            x_own[c].wait_recv()
            if c < BY_Y:
                by_y[c][0].start()
            by_z[c][0].start()
            if c < 4:
                weigh(c)
        for c in range(CHUNKS, 4):
            weigh(c)

    if WEIGH_FIRST:
        when(jnp.logical_not(has_far), weigh_all)
    loads[0].wait()

    def mix(i, number):
        mate_copies[i].wait_recv()
        where = part(number)
        source = choose(own_s[where, :], mate_s[where, :], far_s[where, :])
        mixed[where, :] = jnp.dot(source, rm[...], preferred_element_type=F32).astype(BF16)

    mix(0, q_own)

    @pl.when(has_far)
    def _():
        x_diagonal.wait_recv()

    mix(1, q_d)

    @pl.when(has_far)
    def _():
        for copy in by_z:
            copy[1].wait_recv()

    mix(2, q_z)

    @pl.when(has_far)
    def _():
        for copy in by_y:
            copy[1].wait_recv()
        for copy in x_beside:
            copy.wait_recv()

    mix(3, q_y)

    @pl.when(jnp.logical_not(has_far))
    def _():
        hear(y == 0, 2)
        hear(zlow == 0, 3)

    y_copies, z_copies = [], []
    for k in range(depth):
        start = order[k] * 2 * rows
        give = pl.ds(pl.multiple_of(start + (1 - y) * rows, rows), rows)
        keep = pl.ds(pl.multiple_of(start + y * rows, rows), rows)
        both = jnp.dot(
            jnp.concatenate([lm[give, :], lm[keep, :]], axis=0), mixed[...],
            preferred_element_type=F32,
        )
        y_copies.append([])
        for i in range(pieces):
            y_send[k, i] = both[i * rows_of_piece:(i + 1) * rows_of_piece].astype(BF16)
            copy = remote(
                y_send.at[k, i], y_recv.at[k, i], y_send_sem.at[k, i], y_recv_sem.at[k, i],
                (y_peer, p),
            )
            copy.start()
            y_copies[k].append(copy)
        for i in range(pieces):
            kept[k, i] = both[rows + i * rows_of_piece:rows + (i + 1) * rows_of_piece]

    if not WEIGH_FIRST:
        when(jnp.logical_not(has_far), weigh_all)

    @pl.when(has_far)
    def _():
        site_z.wait_recv()
        site_by_z[0].start()
        site_y.wait_recv()
        site_by_y[0].start()

    def arrival(slot, i):
        return remote(
            z_send.at[0, i], z_recv.at[slot, i], z_send_sem.at[0, i], z_recv_sem.at[slot, i],
            (z_near, p),
        )

    for plane in range(depth):
        higher = jnp.logical_and(plane // 2 != pair, plane > z)
        hear(jnp.logical_and(higher, link_to(plane)), 4 + plane)

    for k in range(depth - 1):
        for i in range(pieces):
            y_copies[k][i].wait_recv()
            kept[k, i] = kept[k, i] + y_recv[k, i].astype(F32)

            @pl.when(acts[k] == 2)
            def _():
                arrival(order[k], i).wait_recv()
                kept[k, i] = kept[k, i] + z_recv[order[k], i].astype(F32)

            z_send[k, i] = kept[k, i].astype(BF16)
            slot = jnp.where(acts[k] == 1, order[k], depth + z)
            peer = jnp.where(acts[k] == 1, z_near, 2 * order[k] + y)
            copy = remote(
                z_send.at[k, i], z_recv.at[slot, i], z_send_sem.at[k, i],
                z_recv_sem.at[slot, i], (peer, p),
            )
            copy.start()
            z_copies.append(copy)

    mate_site.wait_recv()

    @pl.when(has_far)
    def _():
        site_by_z[1].wait_recv()
        site_early.wait_recv()

    early = pl.ds(0, late)
    own_b[early, :] = choose(own_b[early, :], mate_b[early, :], far_b[early, :])
    for i in range(4):
        where = pl.ds(i * quarter, quarter)
        acc[where, :] = jnp.dot(
            weight[where, early], own_b[early, :], preferred_element_type=F32
        )

    last = depth - 1
    for i in range(pieces):
        y_copies[last][i].wait_recv()
        kept[last, i] = kept[last, i] + y_recv[last, i].astype(F32)

    @pl.when(has_far)
    def _():
        for copy in site_late + site_by_y[1:]:
            copy.wait_recv()

    rest = pl.ds(late, width - late)
    lane_mask = (col_ids < source_size).astype(F32)
    tail = choose(own_b[rest, :], mate_b[rest, :], far_b[rest, :])
    for i in range(4):
        where = pl.ds(i * quarter, quarter)
        renewed = acc[where, :] + jnp.dot(
            weight[where, rest], tail, preferred_element_type=F32
        )
        ids = lax.broadcasted_iota(jnp.int32, (quarter, 1), 0) + i * quarter
        renewed = renewed * lane_mask * (ids < own_size).astype(F32)
        new_left[0, 0, where, :] = renewed.astype(BF16)

    keep_cols = (col_ids < own_size).astype(F32)
    for i in range(pieces):
        for plane in range(depth):
            @pl.when(link_from(plane))
            def _():
                arrival(depth + plane, i).wait_recv()
                kept[last, i] = kept[last, i] + z_recv[depth + plane, i].astype(F32)

        ids = lax.broadcasted_iota(jnp.int32, (rows_of_piece, 1), 0) + t * rows + i * rows_of_piece
        keep_rows = (ids < own_size).astype(F32)
        applied[0, pl.ds(i * rows_of_piece, rows_of_piece)] = kept[last, i] * keep_rows * keep_cols

    for copies in y_copies:
        for copy in copies:
            copy.wait_send()
    for copy in z_copies + mate_copies + [mate_site]:
        copy.wait_send()

    @pl.when(has_far)
    def _():
        for copy in x_own + [x_diagonal] + x_beside + x_site:
            copy.wait_send()
        for copy in by_y + by_z + [site_by_z, site_by_y]:
            copy[0].wait_send()


def write_out(applied, new_left, applied_there, new_left_there, sem):
    copies = [
        pltpu.make_async_copy(new_left, new_left_there, sem.at[0]),
        pltpu.make_async_copy(applied, applied_there, sem.at[1]),
    ]
    for copy in copies:
        copy.start()
    for copy in copies:
        copy.wait()


def shards(terms, sectors, state, left_environment, right_environment, site_blocks,
           sector_sizes, term_shift):
    width = state.shape[1]
    rows = width // terms
    depth = terms // 2
    pieces = PIECES if rows % (16 * PIECES) == 0 else 1
    square = pltpu.VMEM((width, width), BF16)
    hbm = pl.BlockSpec(memory_space=pltpu.HBM)
    vmem = pl.BlockSpec(memory_space=pltpu.VMEM)
    dma = pltpu.SemaphoreType.DMA

    def blocks(count, dtype):
        return pltpu.VMEM((count, pieces, rows // pieces, width), dtype)

    outs = (
        ((1, rows, width), F32),
        ((1, 1, width, width), BF16),
    )
    results = pl.pallas_call(
        functools.partial(kernel, terms, sectors),
        out_shape=tuple(pltpu.VMEM(shape, dtype) for shape, dtype in outs),
        in_specs=[hbm] * 6,
        out_specs=(vmem, vmem),
        scratch_shapes=[square] * 11 + [
            pltpu.VMEM((width, width), F32),
            blocks(depth, F32),
            blocks(depth, BF16),
            blocks(depth, BF16),
            blocks(depth, BF16),
            blocks(2 * depth, BF16),
            pltpu.SMEM((sectors,), jnp.int32), pltpu.SMEM((1,), jnp.int32),
            dma((6,)), dma((5,)), dma((5,)), dma((CHUNKS + 7,)), dma((CHUNKS + 7,)),
            dma((2 * CHUNKS + 3,)), dma((2 * CHUNKS + 3,)),
            dma((depth, pieces)), dma((depth, pieces)), dma((depth, pieces)),
            dma((2 * depth, pieces)),
            pltpu.SemaphoreType.REGULAR((4 + depth,)),
        ],
        compiler_params=pltpu.CompilerParams(
            collective_id=0, has_side_effects=True, vmem_limit_bytes=62500 * 1024
        ),
    )(state, left_environment, right_environment, site_blocks, sector_sizes, term_shift)
    return pl.pallas_call(
        write_out,
        out_shape=tuple(jax.ShapeDtypeStruct(shape, dtype) for shape, dtype in outs),
        in_specs=[vmem, vmem],
        out_specs=(hbm, hbm),
        scratch_shapes=[dma((2,))],
    )(*(pltpu.with_memory_space_constraint(result, pltpu.VMEM) for result in results))


def solution(mesh):
    placed = (
        P("sec", None, None),
        P("term", "sec", None, None),
        P("term", "sec", None, None),
        P("sec", None, None),
        P(),
        P("term"),
    )
    return jax.shard_map(
        functools.partial(shards, mesh.shape["term"], mesh.shape["sec"]),
        mesh=mesh,
        in_specs=placed,
        out_specs=(P("sec", "term", None), P("term", "sec", None, None)),
        check_vma=False,
    )
```

```python
import functools

import jax
import jax.numpy as jnp
from jax import lax
from jax.experimental import pallas as pl
from jax.experimental.pallas import tpu as pltpu
from jax.sharding import PartitionSpec as P

MESH = pl.DeviceIdType.MESH
BF16 = jnp.bfloat16
F32 = jnp.float32
CHUNKS = 4
BY_Y = 2
SHARE = 2
LOADS_FIRST = 0
MATE_FIRST = 0
APART = 4
MIX_APART = 1
WRITES = 1
UPWARD = 1
BESIDE = 3
EARLY = 1
DIRECT = (0, 2)
RANK = (1, 0, 2)
WEIGH_FIRST = 0
PIECES = 2


def pick(number, table):
    out = jnp.int32(table[0])
    for i, entry in enumerate(table):
        if i:
            out = jnp.where(number == i, entry, out)
    return out


def hands_over(z, d, direct):
    if z // 2 == d // 2 or (z % 2 == 0) == (d < z):
        return False
    return direct == 0 or direct == 2 and (d % 2 == 1) == (d < z)


def plan(z, depth, direct):
    mate = z + 1 - 2 * (z % 2)
    steps = []
    for d in range(depth):
        if d != z:
            act = 1 if hands_over(z, d, direct) else 0
            if z // 2 != d // 2 and hands_over(mate, d, direct):
                act = 2
            steps.append((RANK[act], d if UPWARD else -abs(d - z), d, act))
    return [(d, act) for _, _, d, act in sorted(steps)]


def kernel(
    terms, sectors,
    state, left, right, site, sizes_there, shift_there,
    applied, new_left,
    own_s, own_b, lm, rm, mate_s, far_s, mate_b, far_b, bt, mixed, weight,
    acc, kept, y_send, y_recv, z_send, z_recv,
    sizes, shift, local_sem, mate_send, mate_recv, x_send_sem, x_recv_sem, relay_send, relay_recv,
    y_send_sem, y_recv_sem, z_send_sem, z_recv_sem, in_sem,
):
    width = own_s.shape[0]
    depth = terms // 2
    rows = width // terms
    pieces, rows_of_piece = y_send.shape[1], y_send.shape[2]
    quarter = width // 4
    chunk = quarter // CHUNKS
    share = width * SHARE // 24
    t, p = lax.axis_index("term"), lax.axis_index("sec")
    z, y = t // 2, t % 2
    odd = p % 2
    mate = p + 1 - 2 * odd
    far = p - 1 + 2 * odd
    has_far = jnp.logical_and(far >= 0, far < sectors)
    far_there = lax.rem(far + sectors, sectors)
    zlow = z % 2
    pair = z // 2
    y_peer = 2 * z + 1 - y
    z_near = 2 * (z + 1 - 2 * zlow) + y
    plans = [[plan(i, depth, direct) for i in range(depth)] for direct in DIRECT]

    def by_plan(table):
        near, away = (pick(z, [table(i, steps) for i, steps in enumerate(kind)]) for kind in plans)
        return jnp.where(has_far, away, near)

    def link_to(j):
        return by_plan(lambda i, steps: int(any(d == j and act != 1 for d, act in steps))) == 1

    def link_from(j):
        near, away = (
            pick(z, [int(any(d == i and act != 1 for d, act in kind[j])) for i in range(depth)])
            for kind in plans
        )
        return jnp.where(has_far, away, near) == 1

    order = [by_plan(lambda i, steps: steps[k][0]) for k in range(depth - 1)] + [z]
    acts = [by_plan(lambda i, steps: steps[k][1]) for k in range(depth - 1)]

    loads = [
        pltpu.make_async_copy(state.at[0], own_s, local_sem.at[0]),
        pltpu.make_async_copy(left.at[0, 0], lm, local_sem.at[1]),
        pltpu.make_async_copy(right.at[0, 0], rm, local_sem.at[2]),
        pltpu.make_async_copy(site.at[0], own_b, local_sem.at[3]),
        pltpu.make_async_copy(sizes_there, sizes, local_sem.at[4]),
        pltpu.make_async_copy(shift_there, shift, local_sem.at[5]),
    ]

    if LOADS_FIRST:
        for load in loads:
            load.start()

    barrier = pltpu.get_barrier_semaphore()
    leads = far > p
    follows = jnp.logical_and(has_far, far < p)
    leads = jnp.logical_and(has_far, leads)

    def when(condition, act):
        @pl.when(condition)
        def _():
            act()

    def greet(condition, device):
        when(condition, lambda: pl.semaphore_signal(
            barrier, inc=1, device_id=device, device_id_type=MESH))

    def answer(condition, device, number):
        when(condition, lambda: pl.semaphore_signal(
            in_sem.at[number], inc=1, device_id=device, device_id_type=MESH))

    def hear(condition, number):
        when(condition, lambda: pl.semaphore_wait(in_sem.at[number], 1))

    greet(leads, (t, far_there))
    greet(odd == 1, (t, mate))
    greet(y == 0, (y_peer, p))
    greet(zlow == 0, (z_near, p))
    below = jnp.int32(0)
    for plane in range(depth):
        apart = plane // 2 != pair
        linked = jnp.logical_and(apart, jnp.logical_or(link_to(plane), link_from(plane)))
        greet(jnp.logical_and(linked, plane > z), (2 * plane + y, p))
        below = below + jnp.where(jnp.logical_and(linked, plane < z), 1, 0)
    greetings = jnp.where(follows, 1, 0) + (1 - odd) + y + zlow + below
    when(greetings > 0, lambda: pl.semaphore_wait(barrier, greetings))
    answer(follows, (t, far_there), 0)
    answer(odd == 0, (t, mate), 1)
    answer(y == 1, (y_peer, p), 2)
    answer(zlow == 1, (z_near, p), 3)
    for plane in range(depth):
        lower = jnp.logical_and(plane // 2 != pair, plane < z)
        answer(jnp.logical_and(lower, link_from(plane)), (2 * plane + y, p), 4 + z)

    def remote(src, dst, send, recv, device):
        return pltpu.make_async_remote_copy(
            src_ref=src, dst_ref=dst, send_sem=send, recv_sem=recv,
            device_id=device, device_id_type=MESH,
        )

    def part(number, first=0, count=CHUNKS):
        return pl.ds(pl.multiple_of(number * quarter + first * chunk, chunk), count * chunk)

    q_own = 2 * zlow + y
    q_y = 2 * zlow + 1 - y
    q_z = 2 * (1 - zlow) + y
    q_d = 2 * (1 - zlow) + 1 - y
    there = (t, far_there)

    x_count = 0

    def cross(array, target, where):
        nonlocal x_count
        copy = remote(
            array.at[0, where], target.at[where],
            x_send_sem.at[x_count], x_recv_sem.at[x_count], there,
        )
        x_count += 1
        return copy

    relay_count = 0

    def relay(target, where, arrives, device):
        nonlocal relay_count
        there_and_back = [
            remote(
                target.at[rows_there], target.at[rows_there],
                relay_send.at[relay_count], relay_recv.at[relay_count], device,
            )
            for rows_there in (where, arrives)
        ]
        relay_count += 1
        return there_and_back

    x_own = [cross(state, far_s, part(q_own, c, 1)) for c in range(CHUNKS)]
    x_diagonal = cross(state, far_s, part(q_d))
    x_beside = [cross(state, far_s, part(q_y, BY_Y, CHUNKS - BY_Y))] if BY_Y < CHUNKS else []
    by_y = [relay(far_s, part(q_own, c, 1), part(q_y, c, 1), (y_peer, p)) for c in range(BY_Y)]
    by_z = [relay(far_s, part(q_own, c, 1), part(q_z, c, 1), (z_near, p)) for c in range(CHUNKS)]
    late = 2 * (width // 3)
    mine = pl.ds(pl.multiple_of(zlow * share, share), share)
    theirs = pl.ds(pl.multiple_of((1 - zlow) * share, share), share)
    beside = width * BESIDE // 24
    mine_y = pl.ds(pl.multiple_of(late + y * beside, 16), beside)
    theirs_y = pl.ds(pl.multiple_of(late + (1 - y) * beside, 16), beside)
    left_over = width - late - 2 * beside
    site_z = cross(site, far_b, mine)
    site_y = cross(site, far_b, mine_y)
    site_early = cross(site, far_b, pl.ds(2 * share, late - 2 * share))
    site_late = [cross(site, far_b, pl.ds(width - left_over, left_over))] if left_over else []
    x_site = [site_z, site_y, site_early] + site_late
    site_by_z = relay(far_b, mine, theirs, (z_near, p))
    site_by_y = relay(far_b, mine_y, theirs_y, (y_peer, p))
    mate_copies = [
        remote(
            state.at[0, part(q)], mate_s.at[part(q)], mate_send.at[i], mate_recv.at[i],
            (t, mate),
        )
        for i, q in enumerate((q_own, q_d, q_z, q_y))
    ]
    mate_site = remote(site.at[0], mate_b, mate_send.at[4], mate_recv.at[4], (t, mate))

    def send_far():
        for copy in x_own + [x_diagonal] + x_beside + x_site:
            copy.start()

    if MATE_FIRST:
        when(odd == 0, lambda: [copy.start() for copy in mate_copies])
    when(follows, send_far)
    if not LOADS_FIRST:
        for load in loads:
            load.start()
    hear(odd == 1, 1)
    if MATE_FIRST:
        when(odd == 1, lambda: [copy.start() for copy in mate_copies])
        mate_site.start()
    else:
        for copy in mate_copies + [mate_site]:
            copy.start()
    if EARLY:
        hear(leads, 0)
        when(leads, send_far)

    loads[4].wait()
    loads[5].wait()
    charge_shift = shift[0]
    own_size = jnp.int32(0)
    source_size = jnp.int32(0)
    for i in range(sectors):
        own_size = own_size + jnp.where(p == i, sizes[i], 0)
        source_size = source_size + jnp.where(p + charge_shift == i, sizes[i], 0)
    towards = charge_shift * (1 - 2 * odd)
    towards = jnp.where(jnp.logical_or(has_far, towards >= 0), towards, 0)

    def choose(own, near, away):
        return jnp.where(towards == 0, own, jnp.where(towards == 1, near, away))

    loads[2].wait()
    row_ids = lax.broadcasted_iota(jnp.int32, (width, 1), 0)
    rm[...] = rm[...] * jnp.where(row_ids < source_size, 1.0, 0.0).astype(BF16)
    loads[1].wait()
    col_ids = lax.broadcasted_iota(jnp.int32, (1, width), 1)
    lm[...] = lm[...] * jnp.where(col_ids < source_size, 1.0, 0.0).astype(BF16)
    if not EARLY:
        hear(leads, 0)
        when(leads, send_far)
    loads[3].wait()
    own_rows = (row_ids < own_size).astype(F32)

    def weigh(i):
        where = pl.ds(i * quarter, quarter)
        weight[where, :] = jnp.dot(
            bt[where, :], lm[...], preferred_element_type=F32
        ).astype(BF16)

    def weigh_all():
        bt[...] = (own_b[...] * own_rows.astype(BF16)).T
        for i in range(4):
            weigh(i)

    @pl.when(has_far)
    def _():
        bt[...] = (own_b[...] * own_rows.astype(BF16)).T
        hear(y == 0, 2)
        hear(zlow == 0, 3)
        for c in range(CHUNKS):
            x_own[c].wait_recv()
            if c < BY_Y:
                by_y[c][0].start()
            by_z[c][0].start()
            if c < 4:
                weigh(c)
        for c in range(CHUNKS, 4):
            weigh(c)

    if WEIGH_FIRST:
        when(jnp.logical_not(has_far), weigh_all)
    loads[0].wait()

    def mix(i, number, *span):
        if i is not None:
            mate_copies[i].wait_recv()
        where = part(number, *span)
        source = choose(own_s[where, :], mate_s[where, :], far_s[where, :])
        mixed[where, :] = jnp.dot(source, rm[...], preferred_element_type=F32).astype(BF16)

    mix(0, q_own)

    @pl.when(has_far)
    def _():
        x_diagonal.wait_recv()

    mix(1, q_d)

    @pl.when(has_far)
    def _():
        for copy in by_z:
            copy[1].wait_recv()

    mix(2, q_z)

    @pl.when(has_far)
    def _():
        for copy in by_y:
            copy[1].wait_recv()
        if not MIX_APART:
            for copy in x_beside:
                copy.wait_recv()

    if MIX_APART and x_beside and by_y:
        mix(3, q_y, 0, BY_Y)

        @pl.when(has_far)
        def _():
            for copy in x_beside:
                copy.wait_recv()

        mix(None, q_y, BY_Y, CHUNKS - BY_Y)
    else:
        mix(3, q_y)

    @pl.when(jnp.logical_not(has_far))
    def _():
        hear(y == 0, 2)
        hear(zlow == 0, 3)

    y_copies, z_copies = [], []
    for k in range(depth):
        start = order[k] * 2 * rows
        give = pl.ds(pl.multiple_of(start + (1 - y) * rows, rows), rows)
        keep = pl.ds(pl.multiple_of(start + y * rows, rows), rows)
        if k < APART:
            given = jnp.dot(lm[give, :], mixed[...], preferred_element_type=F32)
        else:
            both = jnp.dot(
                jnp.concatenate([lm[give, :], lm[keep, :]], axis=0), mixed[...],
                preferred_element_type=F32,
            )
            given, kept_rows = both[:rows], both[rows:]
        y_copies.append([])
        for i in range(pieces):
            y_send[k, i] = given[i * rows_of_piece:(i + 1) * rows_of_piece].astype(BF16)
            copy = remote(
                y_send.at[k, i], y_recv.at[k, i], y_send_sem.at[k, i], y_recv_sem.at[k, i],
                (y_peer, p),
            )
            copy.start()
            y_copies[k].append(copy)
        if k < APART:
            kept_rows = jnp.dot(lm[keep, :], mixed[...], preferred_element_type=F32)
        for i in range(pieces):
            kept[k, i] = kept_rows[i * rows_of_piece:(i + 1) * rows_of_piece]

    if not WEIGH_FIRST:
        when(jnp.logical_not(has_far), weigh_all)

    @pl.when(has_far)
    def _():
        site_z.wait_recv()
        site_by_z[0].start()
        site_y.wait_recv()
        site_by_y[0].start()

    def arrival(slot, i):
        return remote(
            z_send.at[0, i], z_recv.at[slot, i], z_send_sem.at[0, i], z_recv_sem.at[slot, i],
            (z_near, p),
        )

    for plane in range(depth):
        higher = jnp.logical_and(plane // 2 != pair, plane > z)
        hear(jnp.logical_and(higher, link_to(plane)), 4 + plane)

    for k in range(depth - 1):
        for i in range(pieces):
            y_copies[k][i].wait_recv()
            kept[k, i] = kept[k, i] + y_recv[k, i].astype(F32)

            @pl.when(acts[k] == 2)
            def _():
                arrival(order[k], i).wait_recv()
                kept[k, i] = kept[k, i] + z_recv[order[k], i].astype(F32)

            z_send[k, i] = kept[k, i].astype(BF16)
            slot = jnp.where(acts[k] == 1, order[k], depth + z)
            peer = jnp.where(acts[k] == 1, z_near, 2 * order[k] + y)
            copy = remote(
                z_send.at[k, i], z_recv.at[slot, i], z_send_sem.at[k, i],
                z_recv_sem.at[slot, i], (peer, p),
            )
            copy.start()
            z_copies.append(copy)

    mate_site.wait_recv()

    @pl.when(has_far)
    def _():
        site_by_z[1].wait_recv()
        site_early.wait_recv()

    early = pl.ds(0, late)
    own_b[early, :] = choose(own_b[early, :], mate_b[early, :], far_b[early, :])
    for i in range(4):
        where = pl.ds(i * quarter, quarter)
        acc[where, :] = jnp.dot(
            weight[where, early], own_b[early, :], preferred_element_type=F32
        )

    last = depth - 1
    for i in range(pieces):
        y_copies[last][i].wait_recv()
        kept[last, i] = kept[last, i] + y_recv[last, i].astype(F32)

    @pl.when(has_far)
    def _():
        for copy in site_late + site_by_y[1:]:
            copy.wait_recv()

    rest = pl.ds(late, width - late)
    lane_mask = (col_ids < source_size).astype(F32)
    tail = choose(own_b[rest, :], mate_b[rest, :], far_b[rest, :])
    for i in range(4):
        where = pl.ds(i * quarter, quarter)
        renewed = acc[where, :] + jnp.dot(
            weight[where, rest], tail, preferred_element_type=F32
        )
        ids = lax.broadcasted_iota(jnp.int32, (quarter, 1), 0) + i * quarter
        renewed = renewed * lane_mask * (ids < own_size).astype(F32)
        new_left[0, 0, where, :] = renewed.astype(BF16)

    for copies in y_copies:
        for copy in copies:
            copy.wait_send()
    for copy in z_copies + mate_copies + [mate_site]:
        copy.wait_send()

    @pl.when(has_far)
    def _():
        for copy in x_own + [x_diagonal] + x_beside + x_site:
            copy.wait_send()
        for copy in by_y + by_z + [site_by_z, site_by_y]:
            copy[0].wait_send()

    keep_cols = (col_ids < own_size).astype(F32)
    for i in range(pieces):
        for plane in range(depth):
            @pl.when(link_from(plane))
            def _():
                arrival(depth + plane, i).wait_recv()
                kept[last, i] = kept[last, i] + z_recv[depth + plane, i].astype(F32)

        ids = lax.broadcasted_iota(jnp.int32, (rows_of_piece, 1), 0) + t * rows + i * rows_of_piece
        keep_rows = (ids < own_size).astype(F32)
        applied[0, pl.ds(i * rows_of_piece, rows_of_piece)] = kept[last, i] * keep_rows * keep_cols


def write_out(applied, new_left, applied_there, new_left_there, sem):
    rows = new_left.shape[2] // WRITES
    copies = [pltpu.make_async_copy(applied, applied_there, sem.at[WRITES])]
    for i in range(WRITES):
        where = pl.ds(i * rows, rows)
        copies.append(
            pltpu.make_async_copy(
                new_left.at[0, 0, where], new_left_there.at[0, 0, where], sem.at[i]
            )
        )
    for copy in copies:
        copy.start()
    for copy in copies:
        copy.wait()


def shards(terms, sectors, state, left_environment, right_environment, site_blocks,
           sector_sizes, term_shift):
    width = state.shape[1]
    rows = width // terms
    depth = terms // 2
    pieces = PIECES if rows % (16 * PIECES) == 0 else 1
    square = pltpu.VMEM((width, width), BF16)
    hbm = pl.BlockSpec(memory_space=pltpu.HBM)
    vmem = pl.BlockSpec(memory_space=pltpu.VMEM)
    dma = pltpu.SemaphoreType.DMA

    def blocks(count, dtype):
        return pltpu.VMEM((count, pieces, rows // pieces, width), dtype)

    outs = (
        ((1, rows, width), F32),
        ((1, 1, width, width), BF16),
    )
    results = pl.pallas_call(
        functools.partial(kernel, terms, sectors),
        out_shape=tuple(pltpu.VMEM(shape, dtype) for shape, dtype in outs),
        in_specs=[hbm] * 6,
        out_specs=(vmem, vmem),
        scratch_shapes=[square] * 11 + [
            pltpu.VMEM((width, width), F32),
            blocks(depth, F32),
            blocks(depth, BF16),
            blocks(depth, BF16),
            blocks(depth, BF16),
            blocks(2 * depth, BF16),
            pltpu.SMEM((sectors,), jnp.int32), pltpu.SMEM((1,), jnp.int32),
            dma((6,)), dma((5,)), dma((5,)), dma((CHUNKS + 7,)), dma((CHUNKS + 7,)),
            dma((2 * CHUNKS + 3,)), dma((2 * CHUNKS + 3,)),
            dma((depth, pieces)), dma((depth, pieces)), dma((depth, pieces)),
            dma((2 * depth, pieces)),
            pltpu.SemaphoreType.REGULAR((4 + depth,)),
        ],
        compiler_params=pltpu.CompilerParams(
            collective_id=0, has_side_effects=True, vmem_limit_bytes=62500 * 1024
        ),
    )(state, left_environment, right_environment, site_blocks, sector_sizes, term_shift)
    return pl.pallas_call(
        write_out,
        out_shape=tuple(jax.ShapeDtypeStruct(shape, dtype) for shape, dtype in outs),
        in_specs=[vmem, vmem],
        out_specs=(hbm, hbm),
        scratch_shapes=[dma((WRITES + 1,))],
    )(*(pltpu.with_memory_space_constraint(result, pltpu.VMEM) for result in results))


def solution(mesh):
    placed = (
        P("sec", None, None),
        P("term", "sec", None, None),
        P("term", "sec", None, None),
        P("sec", None, None),
        P(),
        P("term"),
    )
    return jax.shard_map(
        functools.partial(shards, mesh.shape["term"], mesh.shape["sec"]),
        mesh=mesh,
        in_specs=placed,
        out_specs=(P("sec", "term", None), P("term", "sec", None, None)),
        check_vma=False,
    )
```

```python
import functools

import jax
import jax.numpy as jnp
from jax import lax
from jax.experimental import pallas as pl
from jax.experimental.pallas import tpu as pltpu
from jax.sharding import PartitionSpec as P

MESH = pl.DeviceIdType.MESH
BF16 = jnp.bfloat16
F32 = jnp.float32
CHUNKS = 4
BY_Y = 2
SHARE = 2
LOADS_FIRST = 0
MATE_FIRST = 0
APART = 4
MIX_APART = 1
WRITES = 1
UPWARD = 1
BESIDE = 3
EARLY = 1
DIRECT = (2, 2)
RANK = (1, 0, 2)
WEIGH_FIRST = 0
PIECES = 2


def pick(number, table):
    out = jnp.int32(table[0])
    for i, entry in enumerate(table):
        if i:
            out = jnp.where(number == i, entry, out)
    return out


def hands_over(z, d, direct):
    if z // 2 == d // 2 or (z % 2 == 0) == (d < z):
        return False
    return direct == 0 or direct == 2 and (d % 2 == 1) == (d < z)


def plan(z, depth, direct):
    mate = z + 1 - 2 * (z % 2)
    steps = []
    for d in range(depth):
        if d != z:
            act = 1 if hands_over(z, d, direct) else 0
            if z // 2 != d // 2 and hands_over(mate, d, direct):
                act = 2
            steps.append((RANK[act], d if UPWARD else -abs(d - z), d, act))
    return [(d, act) for _, _, d, act in sorted(steps)]


def kernel(
    terms, sectors,
    state, left, right, site, sizes_there, shift_there,
    applied, new_left,
    own_s, own_b, lm, rm, mate_s, far_s, mate_b, far_b, bt, mixed, weight,
    acc, kept, y_send, y_recv, z_send, z_recv,
    sizes, shift, local_sem, mate_send, mate_recv, x_send_sem, x_recv_sem, relay_send, relay_recv,
    y_send_sem, y_recv_sem, z_send_sem, z_recv_sem, in_sem,
):
    width = own_s.shape[0]
    depth = terms // 2
    rows = width // terms
    pieces, rows_of_piece = y_send.shape[1], y_send.shape[2]
    quarter = width // 4
    chunk = quarter // CHUNKS
    share = width * SHARE // 24
    t, p = lax.axis_index("term"), lax.axis_index("sec")
    z, y = t // 2, t % 2
    odd = p % 2
    mate = p + 1 - 2 * odd
    far = p - 1 + 2 * odd
    has_far = jnp.logical_and(far >= 0, far < sectors)
    far_there = lax.rem(far + sectors, sectors)
    zlow = z % 2
    pair = z // 2
    y_peer = 2 * z + 1 - y
    z_near = 2 * (z + 1 - 2 * zlow) + y
    plans = [[plan(i, depth, direct) for i in range(depth)] for direct in DIRECT]

    def by_plan(table):
        near, away = (pick(z, [table(i, steps) for i, steps in enumerate(kind)]) for kind in plans)
        return jnp.where(has_far, away, near)

    def link_to(j):
        return by_plan(lambda i, steps: int(any(d == j and act != 1 for d, act in steps))) == 1

    def link_from(j):
        near, away = (
            pick(z, [int(any(d == i and act != 1 for d, act in kind[j])) for i in range(depth)])
            for kind in plans
        )
        return jnp.where(has_far, away, near) == 1

    order = [by_plan(lambda i, steps: steps[k][0]) for k in range(depth - 1)] + [z]
    acts = [by_plan(lambda i, steps: steps[k][1]) for k in range(depth - 1)]

    loads = [
        pltpu.make_async_copy(state.at[0], own_s, local_sem.at[0]),
        pltpu.make_async_copy(left.at[0, 0], lm, local_sem.at[1]),
        pltpu.make_async_copy(right.at[0, 0], rm, local_sem.at[2]),
        pltpu.make_async_copy(site.at[0], own_b, local_sem.at[3]),
        pltpu.make_async_copy(sizes_there, sizes, local_sem.at[4]),
        pltpu.make_async_copy(shift_there, shift, local_sem.at[5]),
    ]

    if LOADS_FIRST:
        for load in loads:
            load.start()

    barrier = pltpu.get_barrier_semaphore()
    leads = far > p
    follows = jnp.logical_and(has_far, far < p)
    leads = jnp.logical_and(has_far, leads)

    def when(condition, act):
        @pl.when(condition)
        def _():
            act()

    def greet(condition, device):
        when(condition, lambda: pl.semaphore_signal(
            barrier, inc=1, device_id=device, device_id_type=MESH))

    def answer(condition, device, number):
        when(condition, lambda: pl.semaphore_signal(
            in_sem.at[number], inc=1, device_id=device, device_id_type=MESH))

    def hear(condition, number):
        when(condition, lambda: pl.semaphore_wait(in_sem.at[number], 1))

    greet(leads, (t, far_there))
    greet(odd == 1, (t, mate))
    greet(y == 0, (y_peer, p))
    greet(zlow == 0, (z_near, p))
    below = jnp.int32(0)
    for plane in range(depth):
        apart = plane // 2 != pair
        linked = jnp.logical_and(apart, jnp.logical_or(link_to(plane), link_from(plane)))
        greet(jnp.logical_and(linked, plane > z), (2 * plane + y, p))
        below = below + jnp.where(jnp.logical_and(linked, plane < z), 1, 0)
    greetings = jnp.where(follows, 1, 0) + (1 - odd) + y + zlow + below
    when(greetings > 0, lambda: pl.semaphore_wait(barrier, greetings))
    answer(follows, (t, far_there), 0)
    answer(odd == 0, (t, mate), 1)
    answer(y == 1, (y_peer, p), 2)
    answer(zlow == 1, (z_near, p), 3)
    for plane in range(depth):
        lower = jnp.logical_and(plane // 2 != pair, plane < z)
        answer(jnp.logical_and(lower, link_from(plane)), (2 * plane + y, p), 4 + z)

    def remote(src, dst, send, recv, device):
        return pltpu.make_async_remote_copy(
            src_ref=src, dst_ref=dst, send_sem=send, recv_sem=recv,
            device_id=device, device_id_type=MESH,
        )

    def part(number, first=0, count=CHUNKS):
        return pl.ds(pl.multiple_of(number * quarter + first * chunk, chunk), count * chunk)

    q_own = 2 * zlow + y
    q_y = 2 * zlow + 1 - y
    q_z = 2 * (1 - zlow) + y
    q_d = 2 * (1 - zlow) + 1 - y
    there = (t, far_there)

    x_count = 0

    def cross(array, target, where):
        nonlocal x_count
        copy = remote(
            array.at[0, where], target.at[where],
            x_send_sem.at[x_count], x_recv_sem.at[x_count], there,
        )
        x_count += 1
        return copy

    relay_count = 0

    def relay(target, where, arrives, device):
        nonlocal relay_count
        there_and_back = [
            remote(
                target.at[rows_there], target.at[rows_there],
                relay_send.at[relay_count], relay_recv.at[relay_count], device,
            )
            for rows_there in (where, arrives)
        ]
        relay_count += 1
        return there_and_back

    x_own = [cross(state, far_s, part(q_own, c, 1)) for c in range(CHUNKS)]
    x_diagonal = cross(state, far_s, part(q_d))
    x_beside = [cross(state, far_s, part(q_y, BY_Y, CHUNKS - BY_Y))] if BY_Y < CHUNKS else []
    by_y = [relay(far_s, part(q_own, c, 1), part(q_y, c, 1), (y_peer, p)) for c in range(BY_Y)]
    by_z = [relay(far_s, part(q_own, c, 1), part(q_z, c, 1), (z_near, p)) for c in range(CHUNKS)]
    late = 2 * (width // 3)
    mine = pl.ds(pl.multiple_of(zlow * share, share), share)
    theirs = pl.ds(pl.multiple_of((1 - zlow) * share, share), share)
    beside = width * BESIDE // 24
    mine_y = pl.ds(pl.multiple_of(late + y * beside, 16), beside)
    theirs_y = pl.ds(pl.multiple_of(late + (1 - y) * beside, 16), beside)
    left_over = width - late - 2 * beside
    site_z = cross(site, far_b, mine)
    site_y = cross(site, far_b, mine_y)
    site_early = cross(site, far_b, pl.ds(2 * share, late - 2 * share))
    site_late = [cross(site, far_b, pl.ds(width - left_over, left_over))] if left_over else []
    x_site = [site_z, site_y, site_early] + site_late
    site_by_z = relay(far_b, mine, theirs, (z_near, p))
    site_by_y = relay(far_b, mine_y, theirs_y, (y_peer, p))
    mate_copies = [
        remote(
            state.at[0, part(q)], mate_s.at[part(q)], mate_send.at[i], mate_recv.at[i],
            (t, mate),
        )
        for i, q in enumerate((q_own, q_d, q_z, q_y))
    ]
    mate_site = remote(site.at[0], mate_b, mate_send.at[4], mate_recv.at[4], (t, mate))

    def send_far():
        for copy in x_own + [x_diagonal] + x_beside + x_site:
            copy.start()

    if MATE_FIRST:
        when(odd == 0, lambda: [copy.start() for copy in mate_copies])
    when(follows, send_far)
    if not LOADS_FIRST:
        for load in loads:
            load.start()
    hear(odd == 1, 1)
    if MATE_FIRST:
        when(odd == 1, lambda: [copy.start() for copy in mate_copies])
        mate_site.start()
    else:
        for copy in mate_copies + [mate_site]:
            copy.start()
    if EARLY:
        hear(leads, 0)
        when(leads, send_far)

    loads[4].wait()
    loads[5].wait()
    charge_shift = shift[0]
    own_size = jnp.int32(0)
    source_size = jnp.int32(0)
    for i in range(sectors):
        own_size = own_size + jnp.where(p == i, sizes[i], 0)
        source_size = source_size + jnp.where(p + charge_shift == i, sizes[i], 0)
    towards = charge_shift * (1 - 2 * odd)
    towards = jnp.where(jnp.logical_or(has_far, towards >= 0), towards, 0)

    def choose(own, near, away):
        return jnp.where(towards == 0, own, jnp.where(towards == 1, near, away))

    loads[2].wait()
    row_ids = lax.broadcasted_iota(jnp.int32, (width, 1), 0)
    rm[...] = rm[...] * jnp.where(row_ids < source_size, 1.0, 0.0).astype(BF16)
    loads[1].wait()
    col_ids = lax.broadcasted_iota(jnp.int32, (1, width), 1)
    lm[...] = lm[...] * jnp.where(col_ids < source_size, 1.0, 0.0).astype(BF16)
    if not EARLY:
        hear(leads, 0)
        when(leads, send_far)
    loads[3].wait()
    own_rows = (row_ids < own_size).astype(F32)

    def weigh(i):
        where = pl.ds(i * quarter, quarter)
        weight[where, :] = jnp.dot(
            bt[where, :], lm[...], preferred_element_type=F32
        ).astype(BF16)

    def weigh_all():
        bt[...] = (own_b[...] * own_rows.astype(BF16)).T
        for i in range(4):
            weigh(i)

    @pl.when(has_far)
    def _():
        bt[...] = (own_b[...] * own_rows.astype(BF16)).T
        hear(y == 0, 2)
        hear(zlow == 0, 3)
        for c in range(CHUNKS):
            x_own[c].wait_recv()
            if c < BY_Y:
                by_y[c][0].start()
            by_z[c][0].start()
            if c < 4:
                weigh(c)
        for c in range(CHUNKS, 4):
            weigh(c)

    if WEIGH_FIRST:
        when(jnp.logical_not(has_far), weigh_all)
    loads[0].wait()

    def mix(i, number, *span):
        if i is not None:
            mate_copies[i].wait_recv()
        where = part(number, *span)
        source = choose(own_s[where, :], mate_s[where, :], far_s[where, :])
        mixed[where, :] = jnp.dot(source, rm[...], preferred_element_type=F32).astype(BF16)

    mix(0, q_own)

    @pl.when(has_far)
    def _():
        x_diagonal.wait_recv()

    mix(1, q_d)

    @pl.when(has_far)
    def _():
        for copy in by_z:
            copy[1].wait_recv()

    mix(2, q_z)

    @pl.when(has_far)
    def _():
        for copy in by_y:
            copy[1].wait_recv()
        if not MIX_APART:
            for copy in x_beside:
                copy.wait_recv()

    if MIX_APART and x_beside and by_y:
        mix(3, q_y, 0, BY_Y)

        @pl.when(has_far)
        def _():
            for copy in x_beside:
                copy.wait_recv()

        mix(None, q_y, BY_Y, CHUNKS - BY_Y)
    else:
        mix(3, q_y)

    @pl.when(jnp.logical_not(has_far))
    def _():
        hear(y == 0, 2)
        hear(zlow == 0, 3)

    y_copies, z_copies = [], []
    for k in range(depth):
        start = order[k] * 2 * rows
        give = pl.ds(pl.multiple_of(start + (1 - y) * rows, rows), rows)
        keep = pl.ds(pl.multiple_of(start + y * rows, rows), rows)
        if k < APART:
            given = jnp.dot(lm[give, :], mixed[...], preferred_element_type=F32)
        else:
            both = jnp.dot(
                jnp.concatenate([lm[give, :], lm[keep, :]], axis=0), mixed[...],
                preferred_element_type=F32,
            )
            given, kept_rows = both[:rows], both[rows:]
        y_copies.append([])
        for i in range(pieces):
            y_send[k, i] = given[i * rows_of_piece:(i + 1) * rows_of_piece].astype(BF16)
            copy = remote(
                y_send.at[k, i], y_recv.at[k, i], y_send_sem.at[k, i], y_recv_sem.at[k, i],
                (y_peer, p),
            )
            copy.start()
            y_copies[k].append(copy)
        if k < APART:
            kept_rows = jnp.dot(lm[keep, :], mixed[...], preferred_element_type=F32)
        for i in range(pieces):
            kept[k, i] = kept_rows[i * rows_of_piece:(i + 1) * rows_of_piece]

    if not WEIGH_FIRST:
        when(jnp.logical_not(has_far), weigh_all)

    @pl.when(has_far)
    def _():
        site_z.wait_recv()
        site_by_z[0].start()
        site_y.wait_recv()
        site_by_y[0].start()

    def arrival(slot, i):
        return remote(
            z_send.at[0, i], z_recv.at[slot, i], z_send_sem.at[0, i], z_recv_sem.at[slot, i],
            (z_near, p),
        )

    for plane in range(depth):
        higher = jnp.logical_and(plane // 2 != pair, plane > z)
        hear(jnp.logical_and(higher, link_to(plane)), 4 + plane)

    for k in range(depth - 1):
        for i in range(pieces):
            y_copies[k][i].wait_recv()
            kept[k, i] = kept[k, i] + y_recv[k, i].astype(F32)

            @pl.when(acts[k] == 2)
            def _():
                arrival(order[k], i).wait_recv()
                kept[k, i] = kept[k, i] + z_recv[order[k], i].astype(F32)

            z_send[k, i] = kept[k, i].astype(BF16)
            slot = jnp.where(acts[k] == 1, order[k], depth + z)
            peer = jnp.where(acts[k] == 1, z_near, 2 * order[k] + y)
            copy = remote(
                z_send.at[k, i], z_recv.at[slot, i], z_send_sem.at[k, i],
                z_recv_sem.at[slot, i], (peer, p),
            )
            copy.start()
            z_copies.append(copy)

    mate_site.wait_recv()

    @pl.when(has_far)
    def _():
        site_by_z[1].wait_recv()
        site_early.wait_recv()

    early = pl.ds(0, late)
    own_b[early, :] = choose(own_b[early, :], mate_b[early, :], far_b[early, :])
    for i in range(4):
        where = pl.ds(i * quarter, quarter)
        acc[where, :] = jnp.dot(
            weight[where, early], own_b[early, :], preferred_element_type=F32
        )

    last = depth - 1
    for i in range(pieces):
        y_copies[last][i].wait_recv()
        kept[last, i] = kept[last, i] + y_recv[last, i].astype(F32)

    @pl.when(has_far)
    def _():
        for copy in site_late + site_by_y[1:]:
            copy.wait_recv()

    rest = pl.ds(late, width - late)
    lane_mask = (col_ids < source_size).astype(F32)
    tail = choose(own_b[rest, :], mate_b[rest, :], far_b[rest, :])
    for i in range(4):
        where = pl.ds(i * quarter, quarter)
        renewed = acc[where, :] + jnp.dot(
            weight[where, rest], tail, preferred_element_type=F32
        )
        ids = lax.broadcasted_iota(jnp.int32, (quarter, 1), 0) + i * quarter
        renewed = renewed * lane_mask * (ids < own_size).astype(F32)
        new_left[0, 0, where, :] = renewed.astype(BF16)

    for copies in y_copies:
        for copy in copies:
            copy.wait_send()
    for copy in z_copies + mate_copies + [mate_site]:
        copy.wait_send()

    @pl.when(has_far)
    def _():
        for copy in x_own + [x_diagonal] + x_beside + x_site:
            copy.wait_send()
        for copy in by_y + by_z + [site_by_z, site_by_y]:
            copy[0].wait_send()

    keep_cols = (col_ids < own_size).astype(F32)
    for i in range(pieces):
        for plane in range(depth):
            @pl.when(link_from(plane))
            def _():
                arrival(depth + plane, i).wait_recv()
                kept[last, i] = kept[last, i] + z_recv[depth + plane, i].astype(F32)

        ids = lax.broadcasted_iota(jnp.int32, (rows_of_piece, 1), 0) + t * rows + i * rows_of_piece
        keep_rows = (ids < own_size).astype(F32)
        applied[0, pl.ds(i * rows_of_piece, rows_of_piece)] = kept[last, i] * keep_rows * keep_cols


def write_out(applied, new_left, applied_there, new_left_there, sem):
    rows = new_left.shape[2] // WRITES
    copies = [pltpu.make_async_copy(applied, applied_there, sem.at[WRITES])]
    for i in range(WRITES):
        where = pl.ds(i * rows, rows)
        copies.append(
            pltpu.make_async_copy(
                new_left.at[0, 0, where], new_left_there.at[0, 0, where], sem.at[i]
            )
        )
    for copy in copies:
        copy.start()
    for copy in copies:
        copy.wait()


def shards(terms, sectors, state, left_environment, right_environment, site_blocks,
           sector_sizes, term_shift):
    width = state.shape[1]
    rows = width // terms
    depth = terms // 2
    pieces = PIECES if rows % (16 * PIECES) == 0 else 1
    square = pltpu.VMEM((width, width), BF16)
    hbm = pl.BlockSpec(memory_space=pltpu.HBM)
    vmem = pl.BlockSpec(memory_space=pltpu.VMEM)
    dma = pltpu.SemaphoreType.DMA

    def blocks(count, dtype):
        return pltpu.VMEM((count, pieces, rows // pieces, width), dtype)

    outs = (
        ((1, rows, width), F32),
        ((1, 1, width, width), BF16),
    )
    results = pl.pallas_call(
        functools.partial(kernel, terms, sectors),
        out_shape=tuple(pltpu.VMEM(shape, dtype) for shape, dtype in outs),
        in_specs=[hbm] * 6,
        out_specs=(vmem, vmem),
        scratch_shapes=[square] * 11 + [
            pltpu.VMEM((width, width), F32),
            blocks(depth, F32),
            blocks(depth, BF16),
            blocks(depth, BF16),
            blocks(depth, BF16),
            blocks(2 * depth, BF16),
            pltpu.SMEM((sectors,), jnp.int32), pltpu.SMEM((1,), jnp.int32),
            dma((6,)), dma((5,)), dma((5,)), dma((CHUNKS + 7,)), dma((CHUNKS + 7,)),
            dma((2 * CHUNKS + 3,)), dma((2 * CHUNKS + 3,)),
            dma((depth, pieces)), dma((depth, pieces)), dma((depth, pieces)),
            dma((2 * depth, pieces)),
            pltpu.SemaphoreType.REGULAR((4 + depth,)),
        ],
        compiler_params=pltpu.CompilerParams(
            collective_id=0, has_side_effects=True, vmem_limit_bytes=62500 * 1024
        ),
    )(state, left_environment, right_environment, site_blocks, sector_sizes, term_shift)
    return pl.pallas_call(
        write_out,
        out_shape=tuple(jax.ShapeDtypeStruct(shape, dtype) for shape, dtype in outs),
        in_specs=[vmem, vmem],
        out_specs=(hbm, hbm),
        scratch_shapes=[dma((WRITES + 1,))],
    )(*(pltpu.with_memory_space_constraint(result, pltpu.VMEM) for result in results))


def solution(mesh):
    placed = (
        P("sec", None, None),
        P("term", "sec", None, None),
        P("term", "sec", None, None),
        P("sec", None, None),
        P(),
        P("term"),
    )
    return jax.shard_map(
        functools.partial(shards, mesh.shape["term"], mesh.shape["sec"]),
        mesh=mesh,
        in_specs=placed,
        out_specs=(P("sec", "term", None), P("term", "sec", None, None)),
        check_vma=False,
    )
```
